32 devices in a mesh: row: 4 (over y, core), col: 8 (over z, x).
Axes of the slice: x: 2, y: 2, z: 4, core: 2. Of those that a mesh axis runs over, the one named last changes fastest.
Arguments:
- couplings: float32 [24576, 24576], P('row', 'col'), may hold values from -0.0390625 to 0.0390625
- diag_terms: float32 [24576], P('col'), may hold values from 1 to 4
- start_block: float32 [3, 24576], P(None, 'col'), may hold values from -6 to 6
Outputs:
- basis_scaled: float32 [2, 3, 24576], P(None, None, 'col')
- coeffs: float32 [2, 2, 3, 3], replicated
The draws below stay inside these ranges and needn't reach their ends.
All inputs are finite; a program needn't handle non-finite values.
Results may differ from the reference program's by a relative error of at most 0.0003.
Values sent between devices are 32-bit elements; how exact they have to be, the bound alone decides.
A program may use at most 128 MiB of HBM per device.

```python
import math
import jax
import jax.numpy as jnp
from jax import lax

RHS = 3
ITERS = 2
M = 24576


def steps_of(stream_key, extent, pieces, low, high):
    def one(position, blocks):
        heights = jax.random.uniform(jax.random.fold_in(jax.random.fold_in(stream_key, 6), position), (blocks,), jnp.float32, low / len(pieces), high / len(pieces))
        return jnp.repeat(jnp.exp(heights), extent[position] // blocks).reshape((-1,) + (1,) * (len(extent) - position - 1))

    factor_of = one(*pieces[0])
    for cut in pieces[1:]:
        factor_of = factor_of * one(*cut)
    return factor_of


def scatter_about(rng, dims, width, reach, pieces=(), kind=jnp.bfloat16):
    drawn = width * jax.random.normal(rng, dims, jnp.float32)
    if pieces:
        drawn = drawn * steps_of(rng, dims, pieces, -0.22, 0.18)
    return jnp.clip(drawn, -reach, reach).astype(kind)


def setup_inputs(seed: int = 0) -> dict:
    key_list = jax.random.split(jax.random.key(seed), 4)
    return {
        "couplings": scatter_about(key_list[0], (M, M), M ** -0.5, 0.0390625, ((0, 4), (1, 8)), jnp.float32),
        "diag_terms": jnp.clip(jnp.exp(math.log(4.0) - 1.3862944 * jax.random.uniform(key_list[1], (M,), jnp.float32) ** steps_of(key_list[1], (M,), ((0, 8),), -0.2, 0.2)), 1.0, 4.0),
        "start_block": scatter_about(key_list[2], (RHS, M), 1.0, 6.0, ((1, 8),), jnp.float32),
    }


def product(a, b):
    return jnp.dot(a.astype(jnp.float32), b.astype(jnp.float32), precision=lax.Precision.HIGHEST, preferred_element_type=jnp.float32)

def orthonormal(block):
    gram_matrix = product(block, block.T)
    factor = jnp.linalg.cholesky(gram_matrix)
    return (jax.scipy.linalg.solve_triangular(factor, block, lower=True), factor)

def reference(couplings, diag_terms, start_block):
    current, first_factor = orthonormal(start_block)
    basis = [current]
    scaled = []
    blocks = []
    root = jnp.sqrt(jnp.float32(M))
    for step in range(ITERS):
        forward = product(couplings, current.T).T
        backward = product(current, couplings)
        image = diag_terms[None, :] * current + 0.5 * (forward + backward)
        prior = jnp.concatenate(basis, 0)
        correlation = product(image, prior.T)
        image = image - product(correlation, prior)
        current, factor = orthonormal(image)
        basis.append(current)
        scaled.append(current * root)
        blocks.append(jnp.stack([correlation[:, 3 * step:3 * step + 3], factor]))
    return (jnp.stack(scaled), jnp.stack(blocks))
```

```python
import functools

import jax
import jax.numpy as jnp
from jax import lax
from jax.experimental import pallas as pl
from jax.experimental.pallas import tpu as pltpu
from jax.sharding import PartitionSpec as P

ITERS = 2
LANES = 128
CONTRACT_LAST = (((1,), (1,)), ((), ()))
CONTRACT_FIRST = (((1,), (0,)), ((), ()))


def split(rows):
    high = lax.reduce_precision(rows, 8, 7)
    low = rows - high
    stacked = jnp.concatenate([high, low], 0).astype(jnp.bfloat16)
    return jnp.pad(stacked, ((0, 16 - stacked.shape[0]), (0, 0)))


def both_kernel(col_ref, row_ref, g_ref, forward_ref, backward_ref):
    g = g_ref[...]
    high = g.astype(jnp.bfloat16)
    low = (g - high.astype(jnp.float32)).astype(jnp.bfloat16)
    col = col_ref[...]
    row = row_ref[...]

    def product(a, b, dims):
        return lax.dot_general(a, b, dims, preferred_element_type=jnp.float32)

    forward_ref[...] = product(col, high, CONTRACT_LAST) + product(col, low, CONTRACT_LAST)

    @pl.when(pl.program_id(0) == 0)
    def _():
        backward_ref[...] = jnp.zeros_like(backward_ref)

    backward_ref[...] += product(row, high, CONTRACT_FIRST) + product(row, low, CONTRACT_FIRST)


def both_products(col_piece, row_piece, couplings):
    height, width = couplings.shape
    tile = min(512, height)
    forward, backward = pl.pallas_call(
        both_kernel,
        grid=(height // tile,),
        in_specs=[
            pl.BlockSpec((16, width), lambda i: (0, 0)),
            pl.BlockSpec((16, tile), lambda i: (0, i)),
            pl.BlockSpec((tile, width), lambda i: (i, 0)),
        ],
        out_specs=[
            pl.BlockSpec((16, tile), lambda i: (0, i)),
            pl.BlockSpec((16, width), lambda i: (0, 0)),
        ],
        out_shape=[
            jax.ShapeDtypeStruct((16, height), jnp.float32),
            jax.ShapeDtypeStruct((16, width), jnp.float32),
        ],
        compiler_params=pltpu.CompilerParams(
            dimension_semantics=("arbitrary",), vmem_limit_bytes=56 * 1024 * 1024
        ),
    )(split(col_piece), split(row_piece), couplings)
    return forward[0:3] + forward[3:6], backward[0:3] + backward[3:6]


def total(x):
    return jnp.sum(jnp.sum(x, axis=0, keepdims=True), axis=1, keepdims=True)


def ortho_kernel(step, *refs):
    if step < 0:
        image_ref, new_ref = refs
        image = [image_ref[i] for i in range(3)]
    else:
        raw_ref, diag_ref = refs[0], refs[1]
        prior_refs = refs[2 : 3 + step]
        new_ref, small_ref = refs[3 + step :]
        diag = diag_ref[...]
        image = [diag * prior_refs[step][i] + raw_ref[i] for i in range(3)]
        row_id = lax.broadcasted_iota(jnp.int32, small_ref.shape, 0)
        col_id = lax.broadcasted_iota(jnp.int32, small_ref.shape, 1)
        small = jnp.zeros(small_ref.shape, jnp.float32)
        taken = list(image)
        for b, prior_ref in enumerate(prior_refs):
            for j in range(3):
                row = prior_ref[j]
                for i in range(3):
                    value = total(image[i] * row)
                    taken[i] = taken[i] - value * row
                    if b == step:
                        small = jnp.where((row_id == i) & (col_id == j), value, small)
        image = taken
    factor = [[None] * 3 for _ in range(3)]
    for i in range(3):
        for j in range(i + 1):
            value = total(image[i] * image[j])
            for k in range(j):
                value = value - factor[i][k] * factor[j][k]
            factor[i][j] = jnp.sqrt(value) if i == j else value / factor[j][j]
            if step >= 0:
                small = jnp.where((row_id == i) & (col_id == j + 3), factor[i][j], small)
    done = []
    for i in range(3):
        row = image[i]
        for k in range(i):
            row = row - factor[i][k] * done[k]
        row = row / factor[i][i]
        done.append(row)
        new_ref[i] = row
    if step >= 0:
        small_ref[...] = small


def ortho(step, *arrays):
    shapes = [jax.ShapeDtypeStruct(arrays[0].shape, jnp.float32)]
    if step >= 0:
        shapes.append(jax.ShapeDtypeStruct((8, LANES), jnp.float32))
    return pl.pallas_call(
        functools.partial(ortho_kernel, step),
        in_specs=[pl.BlockSpec(memory_space=pltpu.VMEM)] * len(arrays),
        out_specs=[pl.BlockSpec(memory_space=pltpu.VMEM)] * len(shapes),
        out_shape=shapes,
        compiler_params=pltpu.CompilerParams(vmem_limit_bytes=32 * 1024 * 1024),
    )(*arrays)


def shards(couplings, diag_terms, start_block):
    row_index = lax.axis_index("row")
    col_index = lax.axis_index("col")
    height, width = couplings.shape
    lines_row, lines_col = height // LANES, width // LANES
    modes = width * lax.axis_size("col")
    lines = modes // LANES
    root = jnp.sqrt(jnp.float32(modes))
    own = jnp.concatenate([start_block, diag_terms[None, :]], 0).reshape(4, lines_col, LANES)
    full = lax.all_gather(own, "col", axis=1, tiled=True)
    diag = full[3]
    (current,) = ortho(-1, full[:3])
    basis = [current]
    scaled = []
    blocks = []
    for step in range(ITERS):
        col_piece = lax.dynamic_slice_in_dim(current, col_index * lines_col, lines_col, 1)
        row_piece = lax.dynamic_slice_in_dim(current, row_index * lines_row, lines_row, 1)
        forward, backward = both_products(
            col_piece.reshape(3, width), row_piece.reshape(3, height), couplings
        )
        placed_forward = lax.dynamic_update_slice_in_dim(
            jnp.zeros((3, lines, LANES), jnp.float32),
            (0.5 * forward).reshape(3, lines_row, LANES), row_index * lines_row, 1,
        )
        placed_backward = lax.dynamic_update_slice_in_dim(
            jnp.zeros((3, lines, LANES), jnp.float32),
            (0.5 * backward).reshape(3, lines_col, LANES), col_index * lines_col, 1,
        )
        raw = lax.psum(placed_forward + placed_backward, ("row", "col"))
        current, small = ortho(step, raw, diag, *basis)
        basis.append(current)
        own_cols = lax.dynamic_slice_in_dim(current, col_index * lines_col, lines_col, 1)
        scaled.append(own_cols.reshape(3, width) * root)
        blocks.append(jnp.stack([small[:3, 0:3], small[:3, 3:6]]))
    return (jnp.stack(scaled), jnp.stack(blocks))


def solution(mesh):
    placed = (P("row", "col"), P("col"), P(None, "col"))
    return jax.shard_map(
        shards, mesh=mesh, in_specs=placed, out_specs=(P(None, None, "col"), P()), check_vma=False
    )
```
